32 devices in a mesh: dp: 8 (over y, x, core), section: 4 (over z).
Axes of the slice: x: 2, y: 2, z: 4, core: 2. Of those that a mesh axis runs over, the one named last changes fastest.
Arguments:
- inputs: bfloat16 [1280, 8192], P('dp'), may hold values from -6 to 6
- cotangent: bfloat16 [1280, 8192], P('dp'), may hold values from -0.625 to 0.625
- weight_in: bfloat16 [4, 8192, 512], P('section'), may hold values from -0.0625 to 0.0625
- weight_out: bfloat16 [4, 8192, 512], P('section'), may hold values from -0.25 to 0.25
- norm_gains: float32 [4, 8192], P('section'), may hold values from 0.1 to 1.9
Outputs:
- in_grad: float32 [4, 8192, 512], P('section', 'dp')
- out_grad: float32 [4, 8192, 512], P('section', 'dp')
- gain_grad: float32 [4, 8192], P('section', 'dp')
The draws below stay inside these ranges and needn't reach their ends.
All inputs are finite; a program needn't handle non-finite values.
Results may differ from the reference program's by a relative error of at most 0.025.
Values may be sent and summed in bfloat16 or wider, within the bound.
A program may use at most 192 MiB of HBM per device.

```python
import jax
import jax.numpy as jnp
from jax import lax

D = 8192
H = 512
SECTIONS = 4
TOK_DEV = 160
TOKENS = 1280
N_DP = 8


def raised(values, stream_key, source, target, shards_of, factor):
    owner, partner = [(jnp.arange(values.shape[position]) // (values.shape[position] // shards_of)).reshape([-1 if axis == position else 1 for axis in range(values.ndim)]) for position in (source, target)]
    chosen = jax.random.permutation(stream_key, shards_of)[partner]
    strong = (owner == chosen) | (owner == (partner + shards_of // 2) % shards_of)
    return jnp.where(strong, factor * values, values)


def shard_levels(stream_key, extent, cuts, low, top_value):
    loudness, own = 1.0, jax.random.fold_in(stream_key, 6)
    for dim, parts in cuts:
        heights = jnp.exp(jax.random.uniform(jax.random.fold_in(own, dim), (parts,), jnp.float32, low / len(cuts), top_value / len(cuts)))
        loudness = loudness * jnp.repeat(heights, extent[dim] // parts).reshape([-1 if axis == dim else 1 for axis in range(len(extent))])
    return loudness


def scatter_about(stream_key, dims, deviation, bound, shards=(), held_as=jnp.bfloat16):
    result = deviation * jax.random.normal(stream_key, dims, jnp.float32)
    if shards:
        result = result * shard_levels(stream_key, dims, shards, -0.22, 0.18)
    return jnp.clip(result, -bound, bound).astype(held_as)


def noise_with(key, shape, deviation, limit, shards, heavy, held_as=jnp.bfloat16):
    result = deviation * jax.random.normal(key, shape, jnp.float32)
    if shards:
        result = result * shard_levels(key, shape, shards, -0.22, 0.18)
    return jnp.clip(raised(result, jax.random.fold_in(key, 3), *heavy), -limit, limit).astype(held_as)


def setup_inputs(seed: int = 0) -> dict:
    key_of = jax.random.split(jax.random.key(seed), 6)
    inputs = scatter_about(key_of[0], (TOKENS, D), 1.0, 6.0, ((0, 8),))
    cotangent = noise_with(key_of[1], (TOKENS, D), (TOKENS ** -0.5), 0.625, ((0, 8),), (0, 1, 8, 2.0))
    weight_in = scatter_about(key_of[2], (SECTIONS, D, H), D ** -0.5, 0.0625, ((0, 4),))
    weight_out = scatter_about(key_of[3], (SECTIONS, D, H), H ** -0.5, 0.25, ((0, 4),))
    norm_gains = jnp.clip(1.0 + 0.18 * jax.random.normal(key_of[4], (SECTIONS, D), jnp.float32), 0.1, 1.9)
    return {"inputs": inputs, "cotangent": cotangent, "weight_in": weight_in, "weight_out": weight_out, "norm_gains": norm_gains}


EPSILON = 1e-05

def normalize(block_rows, gain_row):
    values = block_rows.astype(jnp.float32)
    row_scale = lax.rsqrt(lax.optimization_barrier(jnp.mean(values * values, axis=1, keepdims=True)) + EPSILON)
    normed = (values * row_scale * gain_row).astype(jnp.bfloat16)
    return (values, row_scale, normed)

def layer_forward(block_rows, w_in, w_out, gain_row):
    values, row_scale, normed = normalize(block_rows, gain_row)
    pre_act = jnp.dot(normed, w_in, preferred_element_type=jnp.float32)
    activated = jax.nn.silu(pre_act).astype(jnp.bfloat16)
    branch = lax.dot_general(activated, w_out, (((1,), (1,)), ((), ())), preferred_element_type=jnp.float32)
    return (values + branch).astype(jnp.bfloat16)

def backward_parts(block_rows, upstream, w_in, w_out, gain_row):
    values, row_scale, normed = normalize(block_rows, gain_row)
    pre_act = jnp.dot(normed, w_in, preferred_element_type=jnp.float32)
    activated = jax.nn.silu(pre_act).astype(jnp.bfloat16)
    grad_act = jnp.dot(upstream, w_out, preferred_element_type=jnp.float32)
    sigmoid_pre = jax.nn.sigmoid(pre_act)
    grad_pre = (grad_act * sigmoid_pre * (1.0 + pre_act * (1.0 - sigmoid_pre))).astype(jnp.bfloat16)
    grad_norm = lax.dot_general(grad_pre, w_in, (((1,), (1,)), ((), ())), preferred_element_type=jnp.float32)
    scaled = grad_norm * gain_row
    centered = lax.optimization_barrier(jnp.mean(scaled * values, axis=1, keepdims=True))
    grad_in = (upstream.astype(jnp.float32) + row_scale * scaled - values * row_scale ** 3 * centered).astype(jnp.bfloat16)
    gain_rows = grad_norm * values * row_scale
    return (grad_in, normed, grad_pre, activated, gain_rows)

def column_product(left, right):
    return lax.dot_general(left, right, (((0,), (0,)), ((), ())), preferred_element_type=jnp.float32)

def reference(inputs, cotangent, weight_in, weight_out, norm_gains):
    hidden = [inputs]
    for section_id in range(SECTIONS - 1):
        hidden.append(layer_forward(hidden[-1], weight_in[section_id], weight_out[section_id], norm_gains[section_id]))
    upstream = cotangent
    in_list = [None] * SECTIONS
    out_list = [None] * SECTIONS
    gain_list = [None] * SECTIONS
    for section_id in reversed(range(SECTIONS)):
        grad_in, normed, grad_pre, activated, gain_rows = backward_parts(hidden[section_id], upstream, weight_in[section_id], weight_out[section_id], norm_gains[section_id])
        in_total = jnp.zeros((D, H), jnp.float32)
        out_total = jnp.zeros((D, H), jnp.float32)
        gain_total = jnp.zeros((D,), jnp.float32)
        for replica in range(N_DP):
            low = replica * TOK_DEV
            high = low + TOK_DEV
            in_term = column_product(normed[low:high], grad_pre[low:high])
            in_total = in_total + lax.optimization_barrier(in_term.astype(jnp.bfloat16)).astype(jnp.float32)
            out_term = column_product(upstream[low:high], activated[low:high])
            out_total = out_total + lax.optimization_barrier(out_term.astype(jnp.bfloat16)).astype(jnp.float32)
            gain_term = lax.optimization_barrier(jnp.sum(gain_rows[low:high], axis=0))
            gain_total = gain_total + lax.optimization_barrier(gain_term.astype(jnp.bfloat16)).astype(jnp.float32)
        in_list[section_id] = in_total
        out_list[section_id] = out_total
        gain_list[section_id] = gain_total
        upstream = grad_in
    return (jnp.stack(in_list), jnp.stack(out_list), jnp.stack(gain_list))
```

```python
import functools

import jax
import jax.numpy as jnp
from jax import lax
from jax.experimental import pallas as pl
from jax.experimental.pallas import tpu as pltpu
from jax.sharding import PartitionSpec as P

ROWS = 16
CHUNK = 2048
DELAY = 2
EPSILON = 1e-05
MESH = pl.DeviceIdType.MESH


def nt_dot(left, right):
    return lax.dot_general(
        left, right, (((1,), (1,)), ((), ())), preferred_element_type=jnp.float32
    )


def column_product(left, right):
    return lax.dot_general(
        left, right, (((0,), (0,)), ((), ())), preferred_element_type=jnp.float32
    )


def relay_kernel(
    sections,
    micros,
    x_ref,
    c_ref,
    win_hbm,
    wout_hbm,
    gain_ref,
    n_out,
    g_out,
    act_out,
    du_out,
    gg_out,
    win,
    wout,
    stash,
    up,
    out_f,
    out_b,
    normed,
    pre,
    scale,
    w_sem,
    f_recv,
    b_recv,
    f_send,
    b_send,
    o_sem,
):
    width = stash.shape[2]
    chunks = width // CHUNK
    pos = lax.axis_index("section")
    is_first = pos == 0
    is_last = pos == sections - 1
    not_first = pos > 0
    not_last = pos < sections - 1

    win_copy = pltpu.make_async_copy(win_hbm, win, w_sem.at[0])
    wout_copy = pltpu.make_async_copy(wout_hbm, wout, w_sem.at[1])
    win_copy.start()

    @pl.when(is_first)
    def _():
        @pl.loop(0, micros)
        def _(m):
            pltpu.make_async_copy(x_ref.at[m], stash.at[m], f_recv.at[m]).start()

    wout_copy.start()

    @pl.when(is_last)
    def _():
        @pl.loop(0, micros)
        def _(m):
            pltpu.make_async_copy(c_ref.at[m], up.at[m], b_recv.at[m]).start()

    barrier = pltpu.get_barrier_semaphore()

    @pl.when(not_first)
    def _():
        pl.semaphore_signal(
            barrier, inc=1, device_id={"section": pos - 1}, device_id_type=MESH
        )

    @pl.when(not_last)
    def _():
        pl.semaphore_signal(
            barrier, inc=1, device_id={"section": pos + 1}, device_id_type=MESH
        )

    pl.semaphore_wait(barrier, not_first.astype(jnp.int32) + not_last.astype(jnp.int32))

    gg_out[...] = jnp.zeros_like(gg_out)
    win_copy.wait()
    wout_copy.wait()

    def cols(k):
        return pl.ds(pl.multiple_of(k * CHUNK, CHUNK), CHUNK)

    def send_forward(m):
        return pltpu.make_async_remote_copy(
            src_ref=out_f.at[m],
            dst_ref=stash.at[m],
            send_sem=f_send.at[m],
            recv_sem=f_recv.at[m],
            device_id={"section": pos + 1},
            device_id_type=MESH,
        )

    def send_backward(m):
        return pltpu.make_async_remote_copy(
            src_ref=out_b.at[m],
            dst_ref=up.at[m],
            send_sem=b_send.at[m],
            recv_sem=b_recv.at[m],
            device_id={"section": pos - 1},
            device_id_type=MESH,
        )

    def forward(m):
        pltpu.make_async_copy(stash.at[m], stash.at[m], f_recv.at[m]).wait()

        def add_squares(k, total):
            h = stash[m, :, cols(k)].astype(jnp.float32)
            return total + jnp.sum(h * h, axis=1, keepdims=True)

        total = lax.fori_loop(
            0, chunks, add_squares, jnp.zeros((ROWS, 1), jnp.float32)
        )
        inv = lax.rsqrt(total / width + EPSILON)

        def project(k, acc):
            h = stash[m, :, cols(k)].astype(jnp.float32)
            n = (h * inv * gain_ref[:, cols(k)]).astype(jnp.bfloat16)
            normed[m, :, cols(k)] = n
            return acc + jnp.dot(
                n, win[cols(k), :], preferred_element_type=jnp.float32
            )

        u = lax.fori_loop(
            0, chunks, project, jnp.zeros((ROWS, win.shape[1]), jnp.float32)
        )
        act = (u * jax.nn.sigmoid(u)).astype(jnp.bfloat16)
        pre[m] = u
        scale[m] = jnp.broadcast_to(inv, scale.shape[1:])
        act_out[m] = act

        @pl.when(not_last)
        def _():
            @pl.loop(0, chunks)
            def _(k):
                h = stash[m, :, cols(k)].astype(jnp.float32)
                out_f[m, :, cols(k)] = (h + nt_dot(act, wout[cols(k), :])).astype(
                    jnp.bfloat16
                )

            send_forward(m).start()

    def backward(m):
        pltpu.make_async_copy(up.at[m], up.at[m], b_recv.at[m]).wait()

        def project(k, acc):
            return acc + jnp.dot(
                up[m, :, cols(k)], wout[cols(k), :], preferred_element_type=jnp.float32
            )

        da = lax.fori_loop(
            0, chunks, project, jnp.zeros((ROWS, win.shape[1]), jnp.float32)
        )
        u = pre[m]
        inv = scale[m][:, :1]
        sig = jax.nn.sigmoid(u)
        du = (da * sig * (1.0 + u * (1.0 - sig))).astype(jnp.bfloat16)
        du_out[m] = du
        centered = jnp.sum(du.astype(jnp.float32) * u, axis=1, keepdims=True) / (
            inv * width
        )
        pull = inv * inv * inv * centered

        @pl.loop(0, chunks)
        def _(k):
            h = stash[m, :, cols(k)].astype(jnp.float32)
            dn = nt_dot(du, win[cols(k), :])
            rows = dn * h * inv
            gg_out[:, cols(k)] += rows[:8] + rows[8:]

            @pl.when(not_first)
            def _():
                g = up[m, :, cols(k)].astype(jnp.float32)
                out_b[m, :, cols(k)] = (
                    g + inv * (dn * gain_ref[:, cols(k)]) - h * pull
                ).astype(jnp.bfloat16)

        @pl.when(not_first)
        def _():
            send_backward(m).start()

        pltpu.make_async_copy(normed.at[m], n_out.at[m], o_sem.at[0, m]).start()
        pltpu.make_async_copy(up.at[m], g_out.at[m], o_sem.at[1, m]).start()

    @pl.loop(0, micros + 2 * DELAY * (sections - 1))
    def _(tick):
        mf = tick - DELAY * pos
        mb = tick - DELAY * (2 * (sections - 1) - pos)

        @pl.when((mf >= 0) & (mf < micros))
        def _():
            forward(mf)

        @pl.when((mb >= 0) & (mb < micros))
        def _():
            backward(mb)

    @pl.loop(0, micros)
    def _(m):
        pltpu.make_async_copy(normed.at[m], n_out.at[m], o_sem.at[0, m]).wait()
        pltpu.make_async_copy(up.at[m], g_out.at[m], o_sem.at[1, m]).wait()

        @pl.when(not_last)
        def _():
            send_forward(m).wait_send()

        @pl.when(not_first)
        def _():
            send_backward(m).wait_send()


def local(sections, inputs, cotangent, weight_in, weight_out, norm_gains):
    tokens, width = inputs.shape
    hidden = weight_in.shape[2]
    micros = tokens // ROWS
    wide = jax.ShapeDtypeStruct((micros, ROWS, width), jnp.bfloat16)
    narrow = jax.ShapeDtypeStruct((micros, ROWS, hidden), jnp.bfloat16)
    any_spec = pl.BlockSpec(memory_space=pl.ANY)
    vmem_spec = pl.BlockSpec(memory_space=pltpu.VMEM)
    wide_scratch = pltpu.VMEM((micros, ROWS, width), jnp.bfloat16)
    weight_scratch = pltpu.VMEM((width, hidden), jnp.bfloat16)
    dma = pltpu.SemaphoreType.DMA
    all_norm, all_up, all_act, all_pre, gain_acc = pl.pallas_call(
        functools.partial(relay_kernel, sections, micros),
        out_shape=(
            wide,
            wide,
            narrow,
            narrow,
            jax.ShapeDtypeStruct((8, width), jnp.float32),
        ),
        in_specs=[any_spec] * 4 + [vmem_spec],
        out_specs=(any_spec, any_spec, vmem_spec, vmem_spec, vmem_spec),
        scratch_shapes=[
            weight_scratch,
            weight_scratch,
            wide_scratch,
            wide_scratch,
            wide_scratch,
            wide_scratch,
            wide_scratch,
            pltpu.VMEM((micros, ROWS, hidden), jnp.float32),
            pltpu.VMEM((micros, ROWS, 128), jnp.float32),
            dma((2,)),
            dma((micros,)),
            dma((micros,)),
            dma((micros,)),
            dma((micros,)),
            dma((2, micros)),
        ],
        compiler_params=pltpu.CompilerParams(
            collective_id=0, has_side_effects=True, vmem_limit_bytes=60 * 2**20
        ),
    )(
        inputs.reshape(micros, ROWS, width),
        cotangent.reshape(micros, ROWS, width),
        weight_in[0],
        weight_out[0],
        norm_gains,
    )
    all_norm = all_norm.reshape(tokens, width)
    all_up = all_up.reshape(tokens, width)
    all_act = all_act.reshape(tokens, hidden)
    all_pre = all_pre.reshape(tokens, hidden)
    both_grads = lax.psum_scatter(
        jnp.concatenate(
            [column_product(all_norm, all_pre), column_product(all_up, all_act)], axis=1
        ).astype(jnp.bfloat16),
        "dp",
        scatter_dimension=0,
        tiled=True,
    ).astype(jnp.float32)
    gain_grad = lax.psum_scatter(
        jnp.sum(gain_acc, axis=0).astype(jnp.bfloat16), "dp", scatter_dimension=0, tiled=True
    ).astype(jnp.float32)
    return (both_grads[:, :hidden][None], both_grads[:, hidden:][None], gain_grad[None])


def solution(mesh):
    return jax.shard_map(
        functools.partial(local, mesh.shape["section"]),
        mesh=mesh,
        in_specs=(
            P("dp", None),
            P("dp", None),
            P("section", None, None),
            P("section", None, None),
            P("section", None),
        ),
        out_specs=(P("section", "dp", None), P("section", "dp", None), P("section", "dp")),
        check_vma=False,
    )
```

```python
import functools

import jax
import jax.numpy as jnp
from jax import lax
from jax.experimental import pallas as pl
from jax.experimental.pallas import tpu as pltpu
from jax.sharding import PartitionSpec as P

ROWS = 16
CHUNK = 2048
DELAY = 2
EPSILON = 1e-05
MESH = pl.DeviceIdType.MESH


def nt_dot(left, right):
    return lax.dot_general(
        left, right, (((1,), (1,)), ((), ())), preferred_element_type=jnp.float32
    )


def column_product(left, right):
    return lax.dot_general(
        left, right, (((0,), (0,)), ((), ())), preferred_element_type=jnp.float32
    )


def relay_kernel(
    sections,
    replicas,
    micros,
    x_ref,
    c_ref,
    win_hbm,
    wout_hbm,
    gain_ref,
    all_h,
    all_g,
    all_act,
    all_du,
    all_gain,
    win,
    wout,
    stash,
    up,
    out_f,
    out_b,
    act_buf,
    du_buf,
    gain_acc,
    pre,
    scale,
    w_sem,
    f_recv,
    b_recv,
    f_send,
    b_send,
    x_recv,
    x_send,
):
    width = stash.shape[2]
    chunks = width // CHUNK
    pos = lax.axis_index("section")
    block = width // replicas
    me = lax.axis_index("dp")
    is_first = pos == 0
    is_last = pos == sections - 1
    not_first = pos > 0
    not_last = pos < sections - 1

    win_copy = pltpu.make_async_copy(win_hbm, win, w_sem.at[0])
    wout_copy = pltpu.make_async_copy(wout_hbm, wout, w_sem.at[1])
    win_copy.start()

    @pl.when(is_first)
    def _():
        @pl.loop(0, micros)
        def _(m):
            pltpu.make_async_copy(x_ref.at[m], stash.at[m], f_recv.at[m]).start()

    wout_copy.start()

    @pl.when(is_last)
    def _():
        @pl.loop(0, micros)
        def _(m):
            pltpu.make_async_copy(c_ref.at[m], up.at[m], b_recv.at[m]).start()

    barrier = pltpu.get_barrier_semaphore()

    @pl.when(not_first)
    def _():
        pl.semaphore_signal(
            barrier, inc=1, device_id={"section": pos - 1}, device_id_type=MESH
        )

    @pl.when(not_last)
    def _():
        pl.semaphore_signal(
            barrier, inc=1, device_id={"section": pos + 1}, device_id_type=MESH
        )

    @pl.loop(1, replicas)
    def _(step):
        pl.semaphore_signal(
            barrier,
            inc=1,
            device_id={"dp": lax.rem(me + step, replicas)},
            device_id_type=MESH,
        )

    pl.semaphore_wait(
        barrier,
        replicas - 1 + not_first.astype(jnp.int32) + not_last.astype(jnp.int32),
    )

    gain_acc[...] = jnp.zeros_like(gain_acc)

    def cols(k):
        return pl.ds(pl.multiple_of(k * CHUNK, CHUNK), CHUNK)

    def send_forward(m):
        return pltpu.make_async_remote_copy(
            src_ref=out_f.at[m],
            dst_ref=stash.at[m],
            send_sem=f_send.at[m],
            recv_sem=f_recv.at[m],
            device_id={"section": pos + 1},
            device_id_type=MESH,
        )

    def send_backward(m):
        return pltpu.make_async_remote_copy(
            src_ref=out_b.at[m],
            dst_ref=up.at[m],
            send_sem=b_send.at[m],
            recv_sem=b_recv.at[m],
            device_id={"section": pos - 1},
            device_id_type=MESH,
        )

    def share(kind, src_of, dst):
        pltpu.make_async_copy(src_of(me), dst, x_recv.at[kind]).start()

        @pl.loop(1, replicas)
        def _(step):
            peer = lax.rem(me + step, replicas)
            pltpu.make_async_remote_copy(
                src_ref=src_of(peer),
                dst_ref=dst,
                send_sem=x_send.at[kind],
                recv_sem=x_recv.at[kind],
                device_id={"dp": peer},
                device_id_type=MESH,
            ).start()

    def part(owner):
        return pl.ds(pl.multiple_of(owner * block, block), block)

    def forward(m):
        pltpu.make_async_copy(stash.at[m], stash.at[m], f_recv.at[m]).wait()

        @pl.when(m == 0)
        def _():
            win_copy.wait()

        def project(k, carry):
            total, acc = carry
            h = stash[m, :, cols(k)].astype(jnp.float32)
            scaled = (h * gain_ref[:, cols(k)]).astype(jnp.bfloat16)
            return (
                total + jnp.sum(h * h, axis=1, keepdims=True),
                acc
                + jnp.dot(scaled, win[cols(k), :], preferred_element_type=jnp.float32),
            )

        total, u = lax.fori_loop(
            0,
            chunks,
            project,
            (
                jnp.zeros((ROWS, 1), jnp.float32),
                jnp.zeros((ROWS, win.shape[1]), jnp.float32),
            ),
        )
        inv = lax.rsqrt(total / width + EPSILON)
        u = u * inv
        act = (u * jax.nn.sigmoid(u)).astype(jnp.bfloat16)
        pre[m] = u
        scale[m] = jnp.broadcast_to(inv, scale.shape[1:])
        act_buf[m] = act

        @pl.when(m == 0)
        def _():
            wout_copy.wait()

        @pl.when(not_last)
        def _():
            @pl.loop(0, chunks)
            def _(k):
                h = stash[m, :, cols(k)].astype(jnp.float32)
                out_f[m, :, cols(k)] = (h + nt_dot(act, wout[cols(k), :])).astype(
                    jnp.bfloat16
                )

            send_forward(m).start()

        share(0, lambda owner: stash.at[m, :, part(owner)], all_h.at[me, m])
        share(1, lambda owner: act_buf.at[m], all_act.at[me, m])

    def backward(m):
        pltpu.make_async_copy(up.at[m], up.at[m], b_recv.at[m]).wait()

        def project(k, acc):
            return acc + jnp.dot(
                up[m, :, cols(k)], wout[cols(k), :], preferred_element_type=jnp.float32
            )

        da = lax.fori_loop(
            0, chunks, project, jnp.zeros((ROWS, win.shape[1]), jnp.float32)
        )
        u = pre[m]
        inv = scale[m][:, :1]
        sig = jax.nn.sigmoid(u)
        wide_du = da * sig * (1.0 + u * (1.0 - sig))
        du = wide_du.astype(jnp.bfloat16)
        du_buf[m] = (wide_du * inv).astype(jnp.bfloat16)
        centered = jnp.sum(du.astype(jnp.float32) * u, axis=1, keepdims=True) / (
            inv * width
        )
        pull = inv * inv * inv * centered

        @pl.loop(0, chunks)
        def _(k):
            h = stash[m, :, cols(k)].astype(jnp.float32)
            dn = nt_dot(du, win[cols(k), :])
            rows = dn * h * inv
            gain_acc[:, cols(k)] += rows[:8] + rows[8:]

            @pl.when(not_first)
            def _():
                g = up[m, :, cols(k)].astype(jnp.float32)
                out_b[m, :, cols(k)] = (
                    g + inv * (dn * gain_ref[:, cols(k)]) - h * pull
                ).astype(jnp.bfloat16)

        @pl.when(not_first)
        def _():
            send_backward(m).start()

        share(2, lambda owner: up.at[m, :, part(owner)], all_g.at[me, m])
        share(3, lambda owner: du_buf.at[m], all_du.at[me, m])

    @pl.loop(0, micros + 2 * DELAY * (sections - 1))
    def _(tick):
        mf = tick - DELAY * pos
        mb = tick - DELAY * (2 * (sections - 1) - pos)

        @pl.when((mf >= 0) & (mf < micros))
        def _():
            forward(mf)

        @pl.when((mb >= 0) & (mb < micros))
        def _():
            backward(mb)

    share(4, lambda owner: gain_acc.at[:, part(owner)], all_gain.at[me])

    @pl.loop(0, micros)
    def _(m):
        @pl.when(not_last)
        def _():
            send_forward(m).wait_send()

        @pl.when(not_first)
        def _():
            send_backward(m).wait_send()

    for kind, ref in enumerate((all_h, all_act, all_g, all_du, all_gain)):
        sent = ref.at[pl.ds(0, replicas - 1)]
        pltpu.make_async_copy(sent, sent, x_send.at[kind]).wait()
        pltpu.make_async_copy(ref, ref, x_recv.at[kind]).wait()


def local(sections, replicas, inputs, cotangent, weight_in, weight_out, norm_gains):
    tokens, width = inputs.shape
    hidden = weight_in.shape[2]
    micros = tokens // ROWS
    block = width // replicas
    wide = jax.ShapeDtypeStruct((replicas, micros, ROWS, block), jnp.bfloat16)
    narrow = jax.ShapeDtypeStruct((replicas, micros, ROWS, hidden), jnp.bfloat16)
    any_spec = pl.BlockSpec(memory_space=pl.ANY)
    vmem_spec = pl.BlockSpec(memory_space=pltpu.VMEM)
    wide_scratch = pltpu.VMEM((micros, ROWS, width), jnp.bfloat16)
    weight_scratch = pltpu.VMEM((width, hidden), jnp.bfloat16)
    dma = pltpu.SemaphoreType.DMA
    all_h, all_g, all_act, all_du, all_gain = pl.pallas_call(
        functools.partial(relay_kernel, sections, replicas, micros),
        out_shape=(
            wide,
            wide,
            narrow,
            narrow,
            jax.ShapeDtypeStruct((replicas, 8, block), jnp.float32),
        ),
        in_specs=[any_spec] * 4 + [vmem_spec],
        out_specs=(any_spec,) * 5,
        scratch_shapes=[
            weight_scratch,
            weight_scratch,
            wide_scratch,
            wide_scratch,
            wide_scratch,
            wide_scratch,
            pltpu.VMEM((micros, ROWS, hidden), jnp.bfloat16),
            pltpu.VMEM((micros, ROWS, hidden), jnp.bfloat16),
            pltpu.VMEM((8, width), jnp.float32),
            pltpu.VMEM((micros, ROWS, hidden), jnp.float32),
            pltpu.VMEM((micros, ROWS, 128), jnp.float32),
            dma((2,)),
            dma((micros,)),
            dma((micros,)),
            dma((micros,)),
            dma((micros,)),
            dma((5,)),
            dma((5,)),
        ],
        compiler_params=pltpu.CompilerParams(
            collective_id=0, has_side_effects=True, vmem_limit_bytes=60 * 2**20
        ),
    )(
        inputs.reshape(micros, ROWS, width),
        cotangent.reshape(micros, ROWS, width),
        weight_in[0],
        weight_out[0],
        norm_gains,
    )
    total = replicas * tokens
    own_gain = lax.dynamic_slice_in_dim(
        norm_gains[0], lax.axis_index("dp") * block, block, 0
    )
    in_grad = own_gain[:, None] * column_product(
        all_h.reshape(total, block), all_du.reshape(total, hidden)
    )
    out_grad = column_product(
        all_g.reshape(total, block), all_act.reshape(total, hidden)
    )
    gain_grad = jnp.sum(all_gain, axis=(0, 1))
    return (in_grad[None], out_grad[None], gain_grad[None])


def solution(mesh):
    return jax.shard_map(
        functools.partial(local, mesh.shape["section"], mesh.shape["dp"]),
        mesh=mesh,
        in_specs=(
            P("dp", None),
            P("dp", None),
            P("section", None, None),
            P("section", None, None),
            P("section", None),
        ),
        out_specs=(P("section", "dp", None), P("section", "dp", None), P("section", "dp")),
        check_vma=False,
    )
```

```python
import functools

import jax
import jax.numpy as jnp
from jax import lax
from jax.experimental import pallas as pl
from jax.experimental.pallas import tpu as pltpu
from jax.sharding import PartitionSpec as P

ROWS = 16
CHUNK = 4096
DELAY = 1
EPSILON = 1e-05
MESH = pl.DeviceIdType.MESH


def nt_dot(left, right):
    return lax.dot_general(
        left, right, (((1,), (1,)), ((), ())), preferred_element_type=jnp.float32
    )


def column_product(left, right):
    return lax.dot_general(
        left, right, (((0,), (0,)), ((), ())), preferred_element_type=jnp.float32
    )


def relay_kernel(
    sections,
    replicas,
    micros,
    x_ref,
    c_ref,
    win_hbm,
    wout_hbm,
    gain_ref,
    all_h,
    all_g,
    all_act,
    all_du,
    win,
    wout,
    stash,
    up,
    out_f,
    out_b,
    act_buf,
    du_buf,
    pre,
    scale,
    w_sem,
    f_recv,
    b_recv,
    f_send,
    b_send,
    x_recv,
    x_send,
):
    width = stash.shape[2]
    chunks = width // CHUNK
    pos = lax.axis_index("section")
    block = width // replicas
    me = lax.axis_index("dp")
    is_first = pos == 0
    is_last = pos == sections - 1
    not_first = pos > 0
    not_last = pos < sections - 1

    def cols(k):
        return pl.ds(pl.multiple_of(k * CHUNK, CHUNK), CHUNK)

    win_copy = pltpu.make_async_copy(win_hbm, win, w_sem.at[0])
    wout_copy = pltpu.make_async_copy(wout_hbm, wout, w_sem.at[1])
    win_copy.start()

    @pl.when(is_first)
    def _():
        @pl.loop(0, micros)
        def _(m):
            @pl.loop(0, chunks)
            def _(k):
                pltpu.make_async_copy(
                    x_ref.at[m, :, cols(k)], stash.at[m, :, cols(k)], f_recv.at[m, k]
                ).start()

    wout_copy.start()

    @pl.when(is_last)
    def _():
        @pl.loop(0, micros)
        def _(m):
            @pl.loop(0, chunks)
            def _(k):
                pltpu.make_async_copy(
                    c_ref.at[m, :, cols(k)], up.at[m, :, cols(k)], b_recv.at[m, k]
                ).start()

    barrier = pltpu.get_barrier_semaphore()

    @pl.when(not_first)
    def _():
        pl.semaphore_signal(
            barrier, inc=1, device_id={"section": pos - 1}, device_id_type=MESH
        )

    @pl.when(not_last)
    def _():
        pl.semaphore_signal(
            barrier, inc=1, device_id={"section": pos + 1}, device_id_type=MESH
        )

    @pl.loop(1, replicas)
    def _(step):
        pl.semaphore_signal(
            barrier,
            inc=1,
            device_id={"dp": lax.rem(me + step, replicas)},
            device_id_type=MESH,
        )

    pl.semaphore_wait(
        barrier,
        replicas - 1 + not_first.astype(jnp.int32) + not_last.astype(jnp.int32),
    )

    def send_forward(m, k):
        return pltpu.make_async_remote_copy(
            src_ref=out_f.at[m, :, cols(k)],
            dst_ref=stash.at[m, :, cols(k)],
            send_sem=f_send.at[m, k],
            recv_sem=f_recv.at[m, k],
            device_id={"section": pos + 1},
            device_id_type=MESH,
        )

    def send_backward(m, k):
        return pltpu.make_async_remote_copy(
            src_ref=out_b.at[m, :, cols(k)],
            dst_ref=up.at[m, :, cols(k)],
            send_sem=b_send.at[m, k],
            recv_sem=b_recv.at[m, k],
            device_id={"section": pos - 1},
            device_id_type=MESH,
        )

    def share(kind, src_of, dst):
        pltpu.make_async_copy(src_of(me), dst, x_recv.at[kind]).start()

        @pl.loop(1, replicas)
        def _(step):
            peer = lax.rem(me + step, replicas)
            pltpu.make_async_remote_copy(
                src_ref=src_of(peer),
                dst_ref=dst,
                send_sem=x_send.at[kind],
                recv_sem=x_recv.at[kind],
                device_id={"dp": peer},
                device_id_type=MESH,
            ).start()

    def part(owner):
        return pl.ds(pl.multiple_of(owner * block, block), block)

    def forward(m):
        @pl.when(m == 0)
        def _():
            win_copy.wait()

        def project(k, carry):
            total, acc = carry
            piece = stash.at[m, :, cols(k)]
            pltpu.make_async_copy(piece, piece, f_recv.at[m, k]).wait()
            h = stash[m, :, cols(k)].astype(jnp.float32)
            scaled = (h * gain_ref[:, cols(k)]).astype(jnp.bfloat16)
            return (
                total + jnp.sum(h * h, axis=1, keepdims=True),
                acc
                + jnp.dot(scaled, win[cols(k), :], preferred_element_type=jnp.float32),
            )

        total, u = lax.fori_loop(
            0,
            chunks,
            project,
            (
                jnp.zeros((ROWS, 1), jnp.float32),
                jnp.zeros((ROWS, win.shape[1]), jnp.float32),
            ),
        )
        inv = lax.rsqrt(total / width + EPSILON)
        u = u * inv
        act = (u * jax.nn.sigmoid(u)).astype(jnp.bfloat16)
        pre[m] = u
        scale[m] = jnp.broadcast_to(inv, scale.shape[1:])
        act_buf[m] = act

        @pl.when(m == 0)
        def _():
            wout_copy.wait()

        @pl.when(not_last)
        def _():
            @pl.loop(0, chunks)
            def _(k):
                h = stash[m, :, cols(k)].astype(jnp.float32)
                out_f[m, :, cols(k)] = (h + nt_dot(act, wout[cols(k), :])).astype(
                    jnp.bfloat16
                )
                send_forward(m, k).start()

        share(0, lambda owner: stash.at[m, :, part(owner)], all_h.at[me, m])
        share(1, lambda owner: act_buf.at[m], all_act.at[me, m])

    def backward(m):
        def project(k, acc):
            piece = up.at[m, :, cols(k)]
            pltpu.make_async_copy(piece, piece, b_recv.at[m, k]).wait()
            return acc + jnp.dot(
                up[m, :, cols(k)], wout[cols(k), :], preferred_element_type=jnp.float32
            )

        da = lax.fori_loop(
            0, chunks, project, jnp.zeros((ROWS, win.shape[1]), jnp.float32)
        )
        u = pre[m]
        inv = scale[m][:, :1]
        sig = jax.nn.sigmoid(u)
        wide_du = da * sig * (1.0 + u * (1.0 - sig))
        du = wide_du.astype(jnp.bfloat16)
        du_buf[m] = (wide_du * inv).astype(jnp.bfloat16)
        centered = jnp.sum(du.astype(jnp.float32) * u, axis=1, keepdims=True) / (
            inv * width
        )
        pull = inv * inv * inv * centered

        @pl.when(not_first)
        def _():
            @pl.loop(0, chunks)
            def _(k):
                h = stash[m, :, cols(k)].astype(jnp.float32)
                g = up[m, :, cols(k)].astype(jnp.float32)
                dn = nt_dot(du, win[cols(k), :])
                out_b[m, :, cols(k)] = (
                    g + inv * (dn * gain_ref[:, cols(k)]) - h * pull
                ).astype(jnp.bfloat16)
                send_backward(m, k).start()

        share(2, lambda owner: up.at[m, :, part(owner)], all_g.at[me, m])
        share(3, lambda owner: du_buf.at[m], all_du.at[me, m])

    @pl.loop(0, micros + 2 * DELAY * (sections - 1))
    def _(tick):
        mf = tick - DELAY * pos
        mb = tick - DELAY * (2 * (sections - 1) - pos)

        @pl.when((mf >= 0) & (mf < micros))
        def _():
            forward(mf)

        @pl.when((mb >= 0) & (mb < micros))
        def _():
            backward(mb)

    @pl.loop(0, micros)
    def _(m):
        @pl.loop(0, chunks)
        def _(k):
            @pl.when(not_last)
            def _():
                send_forward(m, k).wait_send()

            @pl.when(not_first)
            def _():
                send_backward(m, k).wait_send()

    for kind, ref in enumerate((all_h, all_act, all_g, all_du)):
        sent = ref.at[pl.ds(0, replicas - 1)]
        pltpu.make_async_copy(sent, sent, x_send.at[kind]).wait()
        pltpu.make_async_copy(ref, ref, x_recv.at[kind]).wait()


def local(sections, replicas, inputs, cotangent, weight_in, weight_out, norm_gains):
    tokens, width = inputs.shape
    hidden = weight_in.shape[2]
    micros = tokens // ROWS
    block = width // replicas
    wide = jax.ShapeDtypeStruct((replicas, micros, ROWS, block), jnp.bfloat16)
    narrow = jax.ShapeDtypeStruct((replicas, micros, ROWS, hidden), jnp.bfloat16)
    any_spec = pl.BlockSpec(memory_space=pl.ANY)
    vmem_spec = pl.BlockSpec(memory_space=pltpu.VMEM)
    wide_scratch = pltpu.VMEM((micros, ROWS, width), jnp.bfloat16)
    weight_scratch = pltpu.VMEM((width, hidden), jnp.bfloat16)
    dma = pltpu.SemaphoreType.DMA
    all_h, all_g, all_act, all_du = pl.pallas_call(
        functools.partial(relay_kernel, sections, replicas, micros),
        out_shape=(
            wide,
            wide,
            narrow,
            narrow,
        ),
        in_specs=[any_spec] * 4 + [vmem_spec],
        out_specs=(any_spec,) * 4,
        scratch_shapes=[
            weight_scratch,
            weight_scratch,
            wide_scratch,
            wide_scratch,
            wide_scratch,
            wide_scratch,
            pltpu.VMEM((micros, ROWS, hidden), jnp.bfloat16),
            pltpu.VMEM((micros, ROWS, hidden), jnp.bfloat16),
            pltpu.VMEM((micros, ROWS, hidden), jnp.float32),
            pltpu.VMEM((micros, ROWS, 128), jnp.float32),
            dma((2,)),
            dma((micros, width // CHUNK)),
            dma((micros, width // CHUNK)),
            dma((micros, width // CHUNK)),
            dma((micros, width // CHUNK)),
            dma((4,)),
            dma((4,)),
        ],
        compiler_params=pltpu.CompilerParams(
            collective_id=0, has_side_effects=True, vmem_limit_bytes=60 * 2**20
        ),
    )(
        inputs.reshape(micros, ROWS, width),
        cotangent.reshape(micros, ROWS, width),
        weight_in[0],
        weight_out[0],
        norm_gains,
    )
    total = replicas * tokens
    own = lax.axis_index("dp") * block
    own_gain = lax.dynamic_slice_in_dim(norm_gains[0], own, block, 0)
    own_rows = lax.dynamic_slice_in_dim(weight_in[0], own, block, 0)
    raw_grad = column_product(
        all_h.reshape(total, block), all_du.reshape(total, hidden)
    )
    in_grad = own_gain[:, None] * raw_grad
    gain_grad = jnp.sum(own_rows.astype(jnp.float32) * raw_grad, axis=1)
    out_grad = column_product(
        all_g.reshape(total, block), all_act.reshape(total, hidden)
    )
    return (in_grad[None], out_grad[None], gain_grad[None])


def solution(mesh):
    return jax.shard_map(
        functools.partial(local, mesh.shape["section"], mesh.shape["dp"]),
        mesh=mesh,
        in_specs=(
            P("dp", None),
            P("dp", None),
            P("section", None, None),
            P("section", None, None),
            P("section", None),
        ),
        out_specs=(P("section", "dp", None), P("section", "dp", None), P("section", "dp")),
        check_vma=False,
    )
```

```python
import functools

import jax
import jax.numpy as jnp
from jax import lax
from jax.experimental import pallas as pl
from jax.experimental.pallas import tpu as pltpu
from jax.sharding import PartitionSpec as P

ROWS = 16
CHUNK = 4096
DELAY = 1
EPSILON = 1e-05
MESH = pl.DeviceIdType.MESH


def nt_dot(left, right):
    return lax.dot_general(
        left, right, (((1,), (1,)), ((), ())), preferred_element_type=jnp.float32
    )


def column_product(left, right):
    return lax.dot_general(
        left, right, (((0,), (0,)), ((), ())), preferred_element_type=jnp.float32
    )


def relay_kernel(
    sections,
    replicas,
    micros,
    x_ref,
    c_ref,
    win_hbm,
    wout_hbm,
    gain_ref,
    all_h,
    all_g,
    all_act,
    all_du,
    own_rows,
    own_gain,
    win,
    wout,
    stash,
    up,
    out_f,
    out_b,
    act_buf,
    du_buf,
    pre,
    scale,
    w_sem,
    f_recv,
    b_recv,
    f_send,
    b_send,
    x_recv,
    x_send,
):
    width = stash.shape[2]
    chunks = width // CHUNK
    pos = lax.axis_index("section")
    block = width // replicas
    me = lax.axis_index("dp")
    is_first = pos == 0
    is_last = pos == sections - 1
    not_first = pos > 0
    not_last = pos < sections - 1

    def cols(k):
        return pl.ds(pl.multiple_of(k * CHUNK, CHUNK), CHUNK)

    def load_in(k):
        return pltpu.make_async_copy(
            win_hbm.at[cols(k), :], win.at[cols(k), :], w_sem.at[k]
        )

    wout_copy = pltpu.make_async_copy(wout_hbm, wout, w_sem.at[chunks])

    @pl.when(is_first)
    def _():
        @pl.loop(0, micros)
        def _(m):
            @pl.loop(0, chunks)
            def _(k):
                pltpu.make_async_copy(
                    x_ref.at[m, :, cols(k)], stash.at[m, :, cols(k)], f_recv.at[m, k]
                ).start()

    @pl.loop(0, chunks)
    def _(k):
        load_in(k).start()

    wout_copy.start()

    @pl.when(is_last)
    def _():
        @pl.loop(0, micros)
        def _(m):
            @pl.loop(0, chunks)
            def _(k):
                pltpu.make_async_copy(
                    c_ref.at[m, :, cols(k)], up.at[m, :, cols(k)], b_recv.at[m, k]
                ).start()

    barrier = pltpu.get_barrier_semaphore()

    @pl.when(not_first)
    def _():
        pl.semaphore_signal(
            barrier, inc=1, device_id={"section": pos - 1}, device_id_type=MESH
        )

    @pl.when(not_last)
    def _():
        pl.semaphore_signal(
            barrier, inc=1, device_id={"section": pos + 1}, device_id_type=MESH
        )

    @pl.loop(1, replicas)
    def _(step):
        pl.semaphore_signal(
            barrier,
            inc=1,
            device_id={"dp": lax.rem(me + step, replicas)},
            device_id_type=MESH,
        )

    pl.semaphore_wait(
        barrier,
        replicas - 1 + not_first.astype(jnp.int32) + not_last.astype(jnp.int32),
    )

    def send_forward(m, k):
        return pltpu.make_async_remote_copy(
            src_ref=out_f.at[m, :, cols(k)],
            dst_ref=stash.at[m, :, cols(k)],
            send_sem=f_send.at[m, k],
            recv_sem=f_recv.at[m, k],
            device_id={"section": pos + 1},
            device_id_type=MESH,
        )

    def send_backward(m, k):
        return pltpu.make_async_remote_copy(
            src_ref=out_b.at[m, :, cols(k)],
            dst_ref=up.at[m, :, cols(k)],
            send_sem=b_send.at[m, k],
            recv_sem=b_recv.at[m, k],
            device_id={"section": pos - 1},
            device_id_type=MESH,
        )

    def share(kind, src_of, dst):
        pltpu.make_async_copy(src_of(me), dst, x_recv.at[kind]).start()

        @pl.loop(1, replicas)
        def _(step):
            peer = lax.rem(me + step, replicas)
            pltpu.make_async_remote_copy(
                src_ref=src_of(peer),
                dst_ref=dst,
                send_sem=x_send.at[kind],
                recv_sem=x_recv.at[kind],
                device_id={"dp": peer},
                device_id_type=MESH,
            ).start()

    def part(owner):
        return pl.ds(pl.multiple_of(owner * block, block), block)

    def forward(m):
        def project(k, carry):
            total, acc = carry
            @pl.when(m == 0)
            def _():
                load_in(k).wait()

            piece = stash.at[m, :, cols(k)]
            pltpu.make_async_copy(piece, piece, f_recv.at[m, k]).wait()
            h = stash[m, :, cols(k)].astype(jnp.float32)
            scaled = (h * gain_ref[:, cols(k)]).astype(jnp.bfloat16)
            return (
                total + jnp.sum(h * h, axis=1, keepdims=True),
                acc
                + jnp.dot(scaled, win[cols(k), :], preferred_element_type=jnp.float32),
            )

        total, u = lax.fori_loop(
            0,
            chunks,
            project,
            (
                jnp.zeros((ROWS, 1), jnp.float32),
                jnp.zeros((ROWS, win.shape[1]), jnp.float32),
            ),
        )
        inv = lax.rsqrt(total / width + EPSILON)
        u = u * inv
        act = (u * jax.nn.sigmoid(u)).astype(jnp.bfloat16)
        pre[m] = u
        scale[m] = jnp.broadcast_to(inv, scale.shape[1:])
        act_buf[m] = act

        @pl.when(m == 0)
        def _():
            wout_copy.wait()

        @pl.when(not_last)
        def _():
            @pl.loop(0, chunks)
            def _(k):
                h = stash[m, :, cols(k)].astype(jnp.float32)
                out_f[m, :, cols(k)] = (h + nt_dot(act, wout[cols(k), :])).astype(
                    jnp.bfloat16
                )
                send_forward(m, k).start()

        share(0, lambda owner: stash.at[m, :, part(owner)], all_h.at[me, m])
        share(1, lambda owner: act_buf.at[m], all_act.at[me, m])

    def backward(m):
        def project(k, acc):
            piece = up.at[m, :, cols(k)]
            pltpu.make_async_copy(piece, piece, b_recv.at[m, k]).wait()
            return acc + jnp.dot(
                up[m, :, cols(k)], wout[cols(k), :], preferred_element_type=jnp.float32
            )

        da = lax.fori_loop(
            0, chunks, project, jnp.zeros((ROWS, win.shape[1]), jnp.float32)
        )
        u = pre[m]
        inv = scale[m][:, :1]
        sig = jax.nn.sigmoid(u)
        wide_du = da * sig * (1.0 + u * (1.0 - sig))
        du = wide_du.astype(jnp.bfloat16)
        du_buf[m] = (wide_du * inv).astype(jnp.bfloat16)
        centered = jnp.sum(du.astype(jnp.float32) * u, axis=1, keepdims=True) / (
            inv * width
        )
        pull = inv * inv * inv * centered

        @pl.when(not_first)
        def _():
            @pl.loop(0, chunks)
            def _(k):
                h = stash[m, :, cols(k)].astype(jnp.float32)
                g = up[m, :, cols(k)].astype(jnp.float32)
                dn = nt_dot(du, win[cols(k), :])
                out_b[m, :, cols(k)] = (
                    g + inv * (dn * gain_ref[:, cols(k)]) - h * pull
                ).astype(jnp.bfloat16)
                send_backward(m, k).start()

        share(2, lambda owner: up.at[m, :, part(owner)], all_g.at[me, m])
        share(3, lambda owner: du_buf.at[m], all_du.at[me, m])

    @pl.loop(0, micros + 2 * DELAY * (sections - 1))
    def _(tick):
        mf = tick - DELAY * pos
        mb = tick - DELAY * (2 * (sections - 1) - pos)

        @pl.when((mf >= 0) & (mf < micros))
        def _():
            forward(mf)

        @pl.when((mb >= 0) & (mb < micros))
        def _():
            backward(mb)

    own_copies = (
        pltpu.make_async_copy(win.at[part(me), :], own_rows, w_sem.at[0]),
        pltpu.make_async_copy(gain_ref.at[:, part(me)], own_gain, w_sem.at[1]),
    )
    own_copies[0].start()
    own_copies[1].start()

    @pl.loop(0, micros)
    def _(m):
        @pl.loop(0, chunks)
        def _(k):
            @pl.when(not_last)
            def _():
                send_forward(m, k).wait_send()

            @pl.when(not_first)
            def _():
                send_backward(m, k).wait_send()

    own_copies[0].wait()
    own_copies[1].wait()
    for kind, ref in enumerate((all_h, all_act, all_g, all_du)):
        sent = ref.at[pl.ds(0, replicas - 1)]
        pltpu.make_async_copy(sent, sent, x_send.at[kind]).wait()
        pltpu.make_async_copy(ref, ref, x_recv.at[kind]).wait()


def local(sections, replicas, inputs, cotangent, weight_in, weight_out, norm_gains):
    tokens, width = inputs.shape
    hidden = weight_in.shape[2]
    micros = tokens // ROWS
    block = width // replicas
    wide = jax.ShapeDtypeStruct((replicas, micros, ROWS, block), jnp.bfloat16)
    narrow = jax.ShapeDtypeStruct((replicas, micros, ROWS, hidden), jnp.bfloat16)
    any_spec = pl.BlockSpec(memory_space=pl.ANY)
    vmem_spec = pl.BlockSpec(memory_space=pltpu.VMEM)
    wide_scratch = pltpu.VMEM((micros, ROWS, width), jnp.bfloat16)
    weight_scratch = pltpu.VMEM((width, hidden), jnp.bfloat16)
    dma = pltpu.SemaphoreType.DMA
    all_h, all_g, all_act, all_du, own_rows, own_gain = pl.pallas_call(
        functools.partial(relay_kernel, sections, replicas, micros),
        out_shape=(
            wide,
            wide,
            narrow,
            narrow,
            jax.ShapeDtypeStruct((block, hidden), jnp.bfloat16),
            jax.ShapeDtypeStruct((1, block), jnp.float32),
        ),
        in_specs=[any_spec] * 4 + [vmem_spec],
        out_specs=(any_spec,) * 6,
        scratch_shapes=[
            weight_scratch,
            weight_scratch,
            wide_scratch,
            wide_scratch,
            wide_scratch,
            wide_scratch,
            pltpu.VMEM((micros, ROWS, hidden), jnp.bfloat16),
            pltpu.VMEM((micros, ROWS, hidden), jnp.bfloat16),
            pltpu.VMEM((micros, ROWS, hidden), jnp.float32),
            pltpu.VMEM((micros, ROWS, 128), jnp.float32),
            dma((width // CHUNK + 2,)),
            dma((micros, width // CHUNK)),
            dma((micros, width // CHUNK)),
            dma((micros, width // CHUNK)),
            dma((micros, width // CHUNK)),
            dma((4,)),
            dma((4,)),
        ],
        compiler_params=pltpu.CompilerParams(
            collective_id=0, has_side_effects=True, vmem_limit_bytes=60 * 2**20
        ),
    )(
        inputs.reshape(micros, ROWS, width),
        cotangent.reshape(micros, ROWS, width),
        weight_in[0],
        weight_out[0],
        norm_gains,
    )
    total = replicas * tokens
    raw_grad = column_product(
        all_h.reshape(total, block), all_du.reshape(total, hidden)
    )
    in_grad = own_gain[0][:, None] * raw_grad
    gain_grad = jnp.sum(own_rows.astype(jnp.float32) * raw_grad, axis=1)
    out_grad = column_product(
        all_g.reshape(total, block), all_act.reshape(total, hidden)
    )
    return (in_grad[None], out_grad[None], gain_grad[None])


def solution(mesh):
    return jax.shard_map(
        functools.partial(local, mesh.shape["section"], mesh.shape["dp"]),
        mesh=mesh,
        in_specs=(
            P("dp", None),
            P("dp", None),
            P("section", None, None),
            P("section", None, None),
            P("section", None),
        ),
        out_specs=(P("section", "dp", None), P("section", "dp", None), P("section", "dp")),
        check_vma=False,
    )
```
